32 devices in a mesh: groups: 2 (over y), dp: 4 (over z), feat: 2 (over core), ens: 2 (over x).
Axes of the slice: x: 2, y: 2, z: 4, core: 2. Of those that a mesh axis runs over, the one named last changes fastest.
Arguments:
- test_feat: bfloat16 [2, 64, 8192], P('ens', 'groups', 'dp'), parts along dimension 1, may hold values from -6 to 6
- kernel_inverse: bfloat16 [2, 8192, 8192], P('ens', 'dp', 'feat'), may hold values from -0.0625 to 0.0625
- train_feat: bfloat16 [2, 1024, 8192], P('ens', 'dp', 'feat'), may hold values from -0.0625 to 0.0625
- residual_weight: float32 [2, 1024], P('ens', 'dp'), may hold values from 0.05 to 1
Outputs:
- scores: float32 [64, 1024], P(('groups', 'feat', 'ens'), 'dp'), parts along dimension 0
The draws below stay inside these ranges and needn't reach their ends.
There are 2 independent parts, one for each index of `groups`. The reference program is written for one: setup_inputs(seed, part) draws one part's arguments, and reference() takes and returns one part's arrays. A program takes and returns all parts, laid end to end along the dimension named above; an argument that names none is the same for every part. Nothing has to cross between parts.
All inputs are finite; a program needn't handle non-finite values.
Results may differ from the reference program's by a relative error of at most 0.0029.
Values may be sent and summed in bfloat16 or wider, within the bound.
A program may use at most 64 MiB of HBM per device.

```python
import math
import jax
import jax.numpy as jnp
from jax import lax

P_SIZE = 8192
MODELS = 2
TEST = 32
NTRAIN = 1024
N_DP = 4


def block_levels(rng, extent, shards, smallest, top_value):
    def one(axis_at, shards_of):
        heights = jax.random.uniform(jax.random.fold_in(jax.random.fold_in(rng, 6), axis_at), (shards_of,), jnp.float32, smallest / len(shards), top_value / len(shards))
        return jnp.repeat(jnp.exp(heights), extent[axis_at] // shards_of).reshape((-1,) + (1,) * (len(extent) - axis_at - 1))

    gain = one(*shards[0])
    for cut in shards[1:]:
        gain = gain * one(*cut)
    return gain


def gaussian(own_key, dims, scale, reach, shards=(), kind=jnp.bfloat16):
    level = block_levels(own_key, dims, shards, -0.22, 0.18) if shards else 1.0
    entries = jax.random.normal(own_key, dims, jnp.float32) * scale * level
    return jnp.minimum(jnp.maximum(entries, -reach), reach).astype(kind)


def setup_inputs(seed: int = 0, part: int = 0) -> dict:
    arg_keys = jax.random.split(jax.random.key(seed), 5)
    own_keys = jax.random.split(jax.random.fold_in(arg_keys[4], part), 5)
    return {
        "test_feat": gaussian(own_keys[0], (MODELS, TEST, P_SIZE), 1.0, 6.0, ((0, 2), (2, 4))),
        "kernel_inverse": gaussian(arg_keys[1], (MODELS, P_SIZE, P_SIZE), P_SIZE ** -0.5, 0.0625, ((0, 2), (1, 4), (2, 2))),
        "train_feat": gaussian(arg_keys[2], (MODELS, NTRAIN, P_SIZE), P_SIZE ** -0.5, 0.0625, ((0, 2), (1, 4), (2, 2))),
        "residual_weight": jnp.clip(jnp.exp(math.log(1.0) - 2.9957323 * jax.random.uniform(arg_keys[3], (MODELS, NTRAIN), jnp.float32) ** block_levels(arg_keys[3], (MODELS, NTRAIN), ((0, 2), (1, 4)), -0.2, 0.2)), 0.05, 1.0),
    }


def project(test_one, inverse_one):
    width = P_SIZE // N_DP

    def add_block(index, total):
        start = (index * width).astype(jnp.int32)
        left = lax.dynamic_slice_in_dim(test_one, start, width, 1)
        right = lax.dynamic_slice_in_dim(inverse_one, start, width, 0)
        term = jnp.dot(left, right, preferred_element_type=jnp.float32)
        return total + term

    total = lax.fori_loop(0, N_DP, add_block, jnp.zeros((TEST, P_SIZE), jnp.float32))
    return total.astype(jnp.bfloat16)


def reference(test_feat, kernel_inverse, train_feat, residual_weight):
    scores = jnp.zeros((TEST, NTRAIN), jnp.float32)
    for model in range(MODELS):
        projected = project(test_feat[model], kernel_inverse[model])
        raw = jnp.dot(projected, train_feat[model].T, preferred_element_type=jnp.float32)
        scores = scores + raw * residual_weight[model][None, :]
    return scores
```

```python
import functools

import jax
import jax.numpy as jnp
from jax import lax
from jax.experimental import pallas as pl
from jax.experimental.pallas import tpu as pltpu
from jax.sharding import PartitionSpec as P

MESH = pl.DeviceIdType.MESH


def kernel(n, feats, models, rounds, test_hbm, inv_hbm, train_hbm, weight_ref, out_ref,
           test_v, inv_v, train_v, part_f, part_b, got, proj, totals, pieces,
           load_sem, inv_sem, rs_send, rs_recv, ag_send, ag_recv, fin_send, fin_recv):
    me = lax.axis_index("dp")
    my_feat, my_model = lax.axis_index("feat"), lax.axis_index("ens")
    rows, depth = test_v.shape
    wide = inv_v.shape[2]
    chunk = wide // n
    finals = feats * models
    spot = my_feat * models + my_model
    each = rows // finals

    test_load = pltpu.make_async_copy(test_hbm.at[0], test_v, load_sem.at[0])
    test_load.start()
    inv_loads = []
    for r in range(rounds):
        load = pltpu.make_async_copy(inv_hbm.at[0, :, pl.ds(r * wide, wide)], inv_v.at[r], inv_sem.at[r])
        load.start()
        inv_loads.append(load)
    train_load = pltpu.make_async_copy(train_hbm.at[0], train_v, load_sem.at[1])
    train_load.start()

    barrier = pltpu.get_barrier_semaphore()
    for k in range(1, n):
        pl.semaphore_signal(barrier, inc=1, device_id={"dp": lax.rem(me + k, n)}, device_id_type=MESH)

    def other(k):
        target = lax.rem(spot + k, finals)
        return target, {"feat": target // models, "ens": lax.rem(target, models)}

    for k in range(1, finals):
        pl.semaphore_signal(barrier, inc=1, device_id=other(k)[1], device_id_type=MESH)
    pl.semaphore_wait(barrier, n - 1 + finals - 1)

    test_load.wait()
    scatters = {}
    gathers = {}

    def project(r):
        inv_loads[r].wait()
        term = jnp.dot(test_v[...], inv_v[r], preferred_element_type=jnp.float32)
        for d in range(n):
            piece = term[:, d * chunk:(d + 1) * chunk]
            part_f[r, d] = piece
            part_b[r, d] = piece.astype(jnp.bfloat16)
        scatters[r] = []
        for k in range(1, n):
            target = lax.rem(me + k, n)
            copy = pltpu.make_async_remote_copy(
                src_ref=part_b.at[r, target], dst_ref=got.at[r, k - 1],
                send_sem=rs_send.at[r, k - 1], recv_sem=rs_recv.at[r, k - 1],
                device_id={"dp": target}, device_id_type=MESH)
            copy.start()
            scatters[r].append(copy)

    def gather(r):
        total = part_f[r, me]
        for k in range(1, n):
            scatters[r][k - 1].wait_recv()
            total = total + got[r, k - 1].astype(jnp.float32)
        proj[r, me] = total.astype(jnp.bfloat16)
        gathers[r] = []
        for k in range(1, n):
            copy = pltpu.make_async_remote_copy(
                src_ref=proj.at[r, me], dst_ref=proj.at[r, me],
                send_sem=ag_send.at[r, k - 1], recv_sem=ag_recv.at[r, k - 1],
                device_id={"dp": lax.rem(me + k, n)}, device_id_type=MESH)
            copy.start()
            gathers[r].append(copy)

    def score(r, raw):
        for copy in gathers[r]:
            copy.wait_recv()
        for d in range(n):
            at = r * wide + d * chunk
            raw = raw + lax.dot_general(
                proj[r, d], train_v[:, at:at + chunk], (((1,), (1,)), ((), ())),
                preferred_element_type=jnp.float32)
        return raw

    raw = jnp.zeros((rows, train_v.shape[0]), jnp.float32)
    for r in range(rounds):
        project(r)
        if r >= 1:
            gather(r - 1)
    gather(rounds - 1)
    train_load.wait()
    for r in range(rounds):
        raw = score(r, raw)

    weighted = raw * weight_ref[...]
    for j in range(finals):
        totals[j] = weighted[j * each:(j + 1) * each]
    last = []
    for k in range(1, finals):
        target, where = other(k)
        copy = pltpu.make_async_remote_copy(
            src_ref=totals.at[target], dst_ref=pieces.at[k - 1],
            send_sem=fin_send.at[k - 1], recv_sem=fin_recv.at[k - 1],
            device_id=where, device_id_type=MESH)
        copy.start()
        last.append(copy)
    done = totals[spot]
    for k in range(1, finals):
        last[k - 1].wait_recv()
        done = done + pieces[k - 1]
    out_ref[...] = done
    for r in range(rounds):
        for copy in scatters[r] + gathers[r]:
            copy.wait_send()
    for copy in last:
        copy.wait_send()


def solution(mesh):
    n, feats, models = mesh.shape["dp"], mesh.shape["feat"], mesh.shape["ens"]
    finals = feats * models

    def shards(test_feat, kernel_inverse, train_feat, residual_weight):
        _, rows, depth = test_feat.shape
        width = kernel_inverse.shape[2]
        cols = train_feat.shape[1]
        rounds = max(1, min(4, width // (n * 256)))
        wide = width // rounds
        chunk = wide // n
        bf16, f32 = jnp.bfloat16, jnp.float32
        any_space = pl.BlockSpec(memory_space=pl.ANY)
        in_vmem = pl.BlockSpec(memory_space=pltpu.VMEM)
        dma = pltpu.SemaphoreType.DMA
        return pl.pallas_call(
            functools.partial(kernel, n, feats, models, rounds),
            out_shape=jax.ShapeDtypeStruct((rows // finals, cols), f32),
            in_specs=[any_space, any_space, any_space, in_vmem],
            out_specs=in_vmem,
            scratch_shapes=[
                pltpu.VMEM((rows, depth), bf16),
                pltpu.VMEM((rounds, depth, wide), bf16),
                pltpu.VMEM((cols, width), bf16),
                pltpu.VMEM((rounds, n, rows, chunk), f32),
                pltpu.VMEM((rounds, n, rows, chunk), bf16),
                pltpu.VMEM((rounds, n - 1, rows, chunk), bf16),
                pltpu.VMEM((rounds, n, rows, chunk), bf16),
                pltpu.VMEM((finals, rows // finals, cols), f32),
                pltpu.VMEM((finals - 1, rows // finals, cols), f32),
                dma((2,)), dma((rounds,)),
                dma((rounds, n - 1)), dma((rounds, n - 1)),
                dma((rounds, n - 1)), dma((rounds, n - 1)),
                dma((finals - 1,)), dma((finals - 1,)),
            ],
            compiler_params=pltpu.CompilerParams(
                collective_id=0, has_side_effects=True, vmem_limit_bytes=60 * 1024 * 1024),
        )(test_feat, kernel_inverse, train_feat, residual_weight)

    in_specs = (
        P("ens", "groups", "dp"),
        P("ens", "dp", "feat"),
        P("ens", "dp", "feat"),
        P("ens", "dp"),
    )
    out_specs = P(("groups", "feat", "ens"), "dp")
    return jax.shard_map(shards, mesh=mesh, in_specs=in_specs, out_specs=out_specs, check_vma=False)
```

```python
import functools

import jax
import jax.numpy as jnp
from jax import lax
from jax.experimental import pallas as pl
from jax.experimental.pallas import tpu as pltpu
from jax.sharding import PartitionSpec as P

MESH = pl.DeviceIdType.MESH


def kernel(n, feats, models, rounds, test_hbm, inv_hbm, train_hbm, weight_ref, out_ref,
           test_v, inv_v, train_v, own, carried, from_outer, from_middle, proj, raw, totals, pieces,
           load_sem, inv_sem, in_send, outer_recv, middle_recv, out_send, out_recv, fin_send, fin_recv):
    me = lax.axis_index("dp")
    my_feat, my_model = lax.axis_index("feat"), lax.axis_index("ens")
    rows = test_v.shape[0]
    wide = inv_v.shape[2]
    finals = feats * models
    spot = my_feat * models + my_model
    each = rows // finals
    half = n // 2
    low = me < half
    inward = jnp.where(low, me + 1, me - 1)
    outward = jnp.where(low, jnp.maximum(me - 1, 0), jnp.minimum(me + 1, n - 1))
    height = jnp.where(low, me, n - 1 - me)
    has_outer = height > 0
    middle = height == half - 1
    lag = 3

    def other(k):
        target = lax.rem(spot + k, finals)
        return target, {"feat": target // models, "ens": lax.rem(target, models)}

    test_load = pltpu.make_async_copy(test_hbm.at[0], test_v, load_sem.at[0])
    test_load.start()
    inv_loads = []
    for r in range(rounds):
        load = pltpu.make_async_copy(inv_hbm.at[0, :, pl.ds(r * wide, wide)], inv_v.at[r], inv_sem.at[r])
        load.start()
        inv_loads.append(load)
    train_load = pltpu.make_async_copy(train_hbm.at[0], train_v, load_sem.at[1])
    train_load.start()

    barrier = pltpu.get_barrier_semaphore()
    pl.semaphore_signal(barrier, inc=1, device_id={"dp": inward}, device_id_type=MESH)

    @pl.when(has_outer)
    def _():
        pl.semaphore_signal(barrier, inc=1, device_id={"dp": outward}, device_id_type=MESH)

    for k in range(1, finals):
        pl.semaphore_signal(barrier, inc=1, device_id=other(k)[1], device_id_type=MESH)
    raw[...] = jnp.zeros_like(raw)
    test_load.wait()
    pl.semaphore_wait(barrier, jnp.where(has_outer, finals + 1, finals))

    def to_next(r):
        return pltpu.make_async_remote_copy(
            src_ref=carried.at[r], dst_ref=from_outer.at[r], send_sem=in_send.at[r],
            recv_sem=outer_recv.at[r], device_id={"dp": inward}, device_id_type=MESH)

    def to_middle(r):
        return pltpu.make_async_remote_copy(
            src_ref=carried.at[r], dst_ref=from_middle.at[r], send_sem=in_send.at[r],
            recv_sem=middle_recv.at[r], device_id={"dp": inward}, device_id_type=MESH)

    def to_outer(r):
        return pltpu.make_async_remote_copy(
            src_ref=proj.at[r], dst_ref=proj.at[r], send_sem=out_send.at[r],
            recv_sem=out_recv.at[r], device_id={"dp": outward}, device_id_type=MESH)

    def project(r):
        inv_loads[r].wait()
        own[r] = jnp.dot(test_v[...], inv_v[r], preferred_element_type=jnp.float32)

    def add_outer(r):
        @pl.when(has_outer)
        def _():
            to_next(r).wait_recv()
            own[r] += from_outer[r].astype(jnp.float32)
        carried[r] = own[r].astype(carried.dtype)

    def pass_out(r):
        @pl.when(has_outer)
        def _():
            to_outer(r).start()

    def score(r):
        raw[...] += lax.dot_general(
            proj[r], train_v[:, r * wide:(r + 1) * wide], (((1,), (1,)), ((), ())),
            preferred_element_type=jnp.float32)

    @pl.when(middle)
    def _():
        def finish(r):
            to_middle(r).wait_recv()
            proj[r] = (own[r] + from_middle[r].astype(jnp.float32)).astype(proj.dtype)
            pass_out(r)
            if r == 0:
                train_load.wait()
            score(r)

        for r in range(rounds):
            project(r)
            add_outer(r)
            to_middle(r).start()
            if r >= lag:
                finish(r - lag)
        for r in range(max(rounds - lag, 0), rounds):
            finish(r)
        for r in range(rounds):
            to_middle(r).wait_send()

    @pl.when(jnp.logical_not(middle))
    def _():
        for r in range(rounds):
            project(r)
            add_outer(r)
            to_next(r).start()
        train_load.wait()
        for r in range(rounds):
            to_outer(r).wait_recv()
            pass_out(r)
            score(r)
        for r in range(rounds):
            to_next(r).wait_send()

    weighted = raw[...] * weight_ref[...]
    for j in range(finals):
        totals[j] = weighted[j * each:(j + 1) * each]
    last = []
    for k in range(1, finals):
        target, where = other(k)
        copy = pltpu.make_async_remote_copy(
            src_ref=totals.at[target], dst_ref=pieces.at[k - 1],
            send_sem=fin_send.at[k - 1], recv_sem=fin_recv.at[k - 1],
            device_id=where, device_id_type=MESH)
        copy.start()
        last.append(copy)
    done = totals[spot]
    for k in range(1, finals):
        last[k - 1].wait_recv()
        done = done + pieces[k - 1]
    out_ref[...] = done

    @pl.when(has_outer)
    def _():
        for r in range(rounds):
            to_outer(r).wait_send()

    for copy in last:
        copy.wait_send()


def solution(mesh):
    n, feats, models = mesh.shape["dp"], mesh.shape["feat"], mesh.shape["ens"]
    finals = feats * models

    def shards(test_feat, kernel_inverse, train_feat, residual_weight):
        _, rows, depth = test_feat.shape
        width = kernel_inverse.shape[2]
        cols = train_feat.shape[1]
        rounds = max(1, min(8, width // 512))
        wide = width // rounds
        bf16, f32 = jnp.bfloat16, jnp.float32
        carry = bf16 if n <= 4 else f32
        any_space = pl.BlockSpec(memory_space=pl.ANY)
        in_vmem = pl.BlockSpec(memory_space=pltpu.VMEM)
        dma = pltpu.SemaphoreType.DMA
        return pl.pallas_call(
            functools.partial(kernel, n, feats, models, rounds),
            out_shape=jax.ShapeDtypeStruct((rows // finals, cols), f32),
            in_specs=[any_space, any_space, any_space, in_vmem],
            out_specs=in_vmem,
            scratch_shapes=[
                pltpu.VMEM((rows, depth), bf16),
                pltpu.VMEM((rounds, depth, wide), bf16),
                pltpu.VMEM((cols, width), bf16),
                pltpu.VMEM((rounds, rows, wide), f32),
                pltpu.VMEM((rounds, rows, wide), carry),
                pltpu.VMEM((rounds, rows, wide), carry),
                pltpu.VMEM((rounds, rows, wide), carry),
                pltpu.VMEM((rounds, rows, wide), bf16),
                pltpu.VMEM((rows, cols), f32),
                pltpu.VMEM((finals, rows // finals, cols), f32),
                pltpu.VMEM((finals - 1, rows // finals, cols), f32),
                dma((2,)), dma((rounds,)),
                dma((rounds,)), dma((rounds,)), dma((rounds,)), dma((rounds,)), dma((rounds,)),
                dma((finals - 1,)), dma((finals - 1,)),
            ],
            compiler_params=pltpu.CompilerParams(
                collective_id=0, has_side_effects=True, vmem_limit_bytes=60 * 1024 * 1024),
        )(test_feat, kernel_inverse, train_feat, residual_weight)

    in_specs = (
        P("ens", "groups", "dp"),
        P("ens", "dp", "feat"),
        P("ens", "dp", "feat"),
        P("ens", "dp"),
    )
    out_specs = P(("groups", "feat", "ens"), "dp")
    return jax.shard_map(shards, mesh=mesh, in_specs=in_specs, out_specs=out_specs, check_vma=False)
```

```python
import functools

import jax
import jax.numpy as jnp
from jax import lax
from jax.experimental import pallas as pl
from jax.experimental.pallas import tpu as pltpu
from jax.sharding import PartitionSpec as P

MESH = pl.DeviceIdType.MESH


def kernel(n, feats, models, rounds, test_hbm, inv_hbm, train_hbm, weight_ref, out_ref,
           test_v, inv_v, train_v, own, carried, from_outer, from_middle, proj, raw, totals, pieces,
           load_sem, inv_sem, in_send, outer_recv, middle_recv, out_send, out_recv, fin_send, fin_recv):
    me = lax.axis_index("dp")
    my_feat, my_model = lax.axis_index("feat"), lax.axis_index("ens")
    rows = test_v.shape[0]
    wide = inv_v.shape[2]
    finals = feats * models
    spot = my_feat * models + my_model
    each = rows // finals
    half = n // 2
    low = me < half
    inward = jnp.where(low, me + 1, me - 1)
    outward = jnp.where(low, jnp.maximum(me - 1, 0), jnp.minimum(me + 1, n - 1))
    height = jnp.where(low, me, n - 1 - me)
    has_outer = height > 0
    middle = height == half - 1
    lag = 4

    def other(k):
        target = lax.rem(spot + k, finals)
        return target, {"feat": target // models, "ens": lax.rem(target, models)}

    test_load = pltpu.make_async_copy(test_hbm.at[0], test_v, load_sem.at[0])
    test_load.start()
    inv_loads = []
    for r in range(rounds):
        load = pltpu.make_async_copy(inv_hbm.at[0, :, pl.ds(r * wide, wide)], inv_v.at[r], inv_sem.at[r])
        load.start()
        inv_loads.append(load)
    train_load = pltpu.make_async_copy(train_hbm.at[0], train_v, load_sem.at[1])
    train_load.start()

    barrier = pltpu.get_barrier_semaphore()
    pl.semaphore_signal(barrier, inc=1, device_id={"dp": inward}, device_id_type=MESH)

    @pl.when(has_outer)
    def _():
        pl.semaphore_signal(barrier, inc=1, device_id={"dp": outward}, device_id_type=MESH)

    for k in range(1, finals):
        pl.semaphore_signal(barrier, inc=1, device_id=other(k)[1], device_id_type=MESH)
    raw[...] = jnp.zeros_like(raw)
    test_load.wait()
    pl.semaphore_wait(barrier, jnp.where(has_outer, finals + 1, finals))

    def to_next(r):
        return pltpu.make_async_remote_copy(
            src_ref=carried.at[r], dst_ref=from_outer.at[r], send_sem=in_send.at[r],
            recv_sem=outer_recv.at[r], device_id={"dp": inward}, device_id_type=MESH)

    def to_middle(r):
        return pltpu.make_async_remote_copy(
            src_ref=carried.at[r], dst_ref=from_middle.at[r], send_sem=in_send.at[r],
            recv_sem=middle_recv.at[r], device_id={"dp": inward}, device_id_type=MESH)

    def to_outer(r):
        return pltpu.make_async_remote_copy(
            src_ref=proj.at[r], dst_ref=proj.at[r], send_sem=out_send.at[r],
            recv_sem=out_recv.at[r], device_id={"dp": outward}, device_id_type=MESH)

    def project(r):
        inv_loads[r].wait()
        own[r] = jnp.dot(test_v[...], inv_v[r], preferred_element_type=jnp.float32)

    def add_outer(r):
        @pl.when(has_outer)
        def _():
            to_next(r).wait_recv()
            own[r] += from_outer[r].astype(jnp.float32)
        carried[r] = own[r].astype(carried.dtype)

    def pass_out(r):
        @pl.when(has_outer)
        def _():
            to_outer(r).start()

    def score(r):
        raw[...] += lax.dot_general(
            proj[r], train_v[:, r * wide:(r + 1) * wide], (((1,), (1,)), ((), ())),
            preferred_element_type=jnp.float32)

    @pl.when(middle)
    def _():
        def finish(r):
            to_middle(r).wait_recv()
            proj[r] = (own[r] + from_middle[r].astype(jnp.float32)).astype(proj.dtype)
            pass_out(r)
            if r == 0:
                train_load.wait()
            score(r)

        for r in range(rounds):
            project(r)
            add_outer(r)
            to_middle(r).start()
            if r >= lag:
                finish(r - lag)
        for r in range(max(rounds - lag, 0), rounds):
            finish(r)
        for r in range(rounds):
            to_middle(r).wait_send()

    @pl.when(jnp.logical_not(middle))
    def _():
        for r in range(rounds):
            project(r)
            add_outer(r)
            to_next(r).start()
        train_load.wait()
        for r in range(rounds):
            to_outer(r).wait_recv()
            pass_out(r)
            score(r)
        for r in range(rounds):
            to_next(r).wait_send()

    weighted = raw[...] * weight_ref[...]
    for j in range(finals):
        totals[j] = weighted[j * each:(j + 1) * each]
    last = []
    for k in range(1, finals):
        target, where = other(k)
        copy = pltpu.make_async_remote_copy(
            src_ref=totals.at[target], dst_ref=pieces.at[k - 1],
            send_sem=fin_send.at[k - 1], recv_sem=fin_recv.at[k - 1],
            device_id=where, device_id_type=MESH)
        copy.start()
        last.append(copy)
    done = totals[spot]
    for k in range(1, finals):
        last[k - 1].wait_recv()
        done = done + pieces[k - 1]
    out_ref[...] = done

    @pl.when(has_outer)
    def _():
        for r in range(rounds):
            to_outer(r).wait_send()

    for copy in last:
        copy.wait_send()


def solution(mesh):
    n, feats, models = mesh.shape["dp"], mesh.shape["feat"], mesh.shape["ens"]
    finals = feats * models

    def shards(test_feat, kernel_inverse, train_feat, residual_weight):
        _, rows, depth = test_feat.shape
        width = kernel_inverse.shape[2]
        cols = train_feat.shape[1]
        rounds = max(1, min(4, width // 512))
        wide = width // rounds
        bf16, f32 = jnp.bfloat16, jnp.float32
        carry = bf16 if n <= 4 else f32
        any_space = pl.BlockSpec(memory_space=pl.ANY)
        in_vmem = pl.BlockSpec(memory_space=pltpu.VMEM)
        dma = pltpu.SemaphoreType.DMA
        return pl.pallas_call(
            functools.partial(kernel, n, feats, models, rounds),
            out_shape=jax.ShapeDtypeStruct((rows // finals, cols), f32),
            in_specs=[any_space, any_space, any_space, in_vmem],
            out_specs=in_vmem,
            scratch_shapes=[
                pltpu.VMEM((rows, depth), bf16),
                pltpu.VMEM((rounds, depth, wide), bf16),
                pltpu.VMEM((cols, width), bf16),
                pltpu.VMEM((rounds, rows, wide), f32),
                pltpu.VMEM((rounds, rows, wide), carry),
                pltpu.VMEM((rounds, rows, wide), carry),
                pltpu.VMEM((rounds, rows, wide), carry),
                pltpu.VMEM((rounds, rows, wide), bf16),
                pltpu.VMEM((rows, cols), f32),
                pltpu.VMEM((finals, rows // finals, cols), f32),
                pltpu.VMEM((finals - 1, rows // finals, cols), f32),
                dma((2,)), dma((rounds,)),
                dma((rounds,)), dma((rounds,)), dma((rounds,)), dma((rounds,)), dma((rounds,)),
                dma((finals - 1,)), dma((finals - 1,)),
            ],
            compiler_params=pltpu.CompilerParams(
                collective_id=0, has_side_effects=True, vmem_limit_bytes=60 * 1024 * 1024),
        )(test_feat, kernel_inverse, train_feat, residual_weight)

    in_specs = (
        P("ens", "groups", "dp"),
        P("ens", "dp", "feat"),
        P("ens", "dp", "feat"),
        P("ens", "dp"),
    )
    out_specs = P(("groups", "feat", "ens"), "dp")
    return jax.shard_map(shards, mesh=mesh, in_specs=in_specs, out_specs=out_specs, check_vma=False)
```
